32 devices in a mesh: prow: 8 (over z, y), pcol: 4 (over x, core).
Axes of the slice: x: 2, y: 2, z: 4, core: 2. Of those that a mesh axis runs over, the one named last changes fastest.
Arguments:
- a_panel: float32 [98304, 512], P('prow', 'pcol'), may hold values from -6 to 6
- u_rows: float32 [512, 98304], P('pcol', 'prow'), may hold values from -0.25 to 0.25
- u_col: float32 [98304, 2048], P('prow', 'pcol'), may hold values from -0.01953125 to 0.01953125
- c_in: float32 [98304, 2048], P('prow', 'pcol'), may hold values from -6 to 6
Outputs:
- c_out: float32 [98304, 2048], P('prow', 'pcol')
The draws below stay inside these ranges and needn't reach their ends.
All inputs are finite; a program needn't handle non-finite values.
Results may differ from the reference program's by a relative error of at most 0.00007.
Values sent between devices are 32-bit elements; how exact they have to be, the bound alone decides.
A program may use at most 192 MiB of HBM per device.

```python
import jax
import jax.numpy as jnp
from jax import lax

N = 98304
SLAB = 2048
KW = 512


def block_scale(own_key, dims, cuts, least, largest):
    level = 1.0
    for axis_at, shards_of in cuts:
        heights = jax.random.uniform(jax.random.fold_in(jax.random.fold_in(own_key, 6), axis_at), (shards_of,), jnp.float32, least / len(cuts), largest / len(cuts))
        level = level * jnp.repeat(jnp.exp(heights), dims[axis_at] // shards_of).reshape((-1,) + (1,) * (len(dims) - 1 - axis_at))
    return level


def scatter_about(stream_key, dims, deviation, bound, split=(), held_as=jnp.bfloat16):
    gain = block_scale(stream_key, dims, split, -0.22, 0.18) if split else 1.0
    entries = jax.random.normal(stream_key, dims, jnp.float32) * deviation * gain
    return jnp.minimum(jnp.maximum(entries, -bound), bound).astype(held_as)


def setup_inputs(seed: int = 0) -> dict:
    arg_keys = jax.random.split(jax.random.key(seed), 5)
    a_panel = scatter_about(arg_keys[0], (N, KW), 1.0, 6.0, ((0, 8), (1, 4)), jnp.float32)
    u_rows = scatter_about(arg_keys[1], (KW, N), KW ** -0.5, 0.25, ((0, 4), (1, 8)), jnp.float32)
    u_col = scatter_about(arg_keys[2], (N, SLAB), N ** -0.5, 0.01953125, ((0, 8), (1, 4)), jnp.float32)
    c_in = scatter_about(arg_keys[3], (N, SLAB), 1.0, 6.0, ((0, 8), (1, 4)), jnp.float32)
    return dict(a_panel=a_panel, u_rows=u_rows, u_col=u_col, c_in=c_in)


def reference(a_panel, u_rows, u_col, c_in):
    inner = jnp.dot(a_panel.T, u_col, precision=lax.Precision.HIGHEST, preferred_element_type=jnp.float32)
    update = jnp.dot(u_rows.T, inner, precision=lax.Precision.HIGHEST, preferred_element_type=jnp.float32)
    return c_in + update
```

```python
import functools

import jax
import jax.numpy as jnp
from jax import lax
from jax.experimental import pallas as pl
from jax.experimental.pallas import tpu as pltpu
from jax.sharding import PartitionSpec as P


UNITS = 24
A_CHUNKS = (6, 6, 6, 6)
U_CHUNKS = (6, 6, 6, 3, 2, 1)
DEPTH = 3
TN = (((0,), (0,)), ((), ()))


def parts(x):
    hi = x.astype(jnp.bfloat16)
    return hi, (x - hi.astype(jnp.float32)).astype(jnp.bfloat16)


def dot3(a_hi, a_lo, b_hi, b_lo):
    dot = functools.partial(lax.dot_general, dimension_numbers=TN, preferred_element_type=jnp.float32)
    return dot(a_hi, b_hi) + (dot(a_lo, b_hi) + dot(a_hi, b_lo))


def inner_kernel(first, *refs):
    blocks, (ucol, before, _, out, mark) = refs[:-5], refs[-5:]

    @pl.when(pl.program_id(0) == 0)
    def _():
        mark[...] = jnp.zeros_like(mark)
        out[...] = jnp.zeros_like(out) if first else before[...]

    u_hi, u_lo = parts(ucol[...])
    width = blocks[0].shape[1]
    for k, block in enumerate(blocks):
        a_hi, a_lo = parts(block[...])
        out[pl.ds(k * width, width), :] += dot3(a_hi, a_lo, u_hi, u_lo)


def update_kernel(*refs):
    blocks, (inner, c_in, _, _, out, mark, i_hi, i_lo) = refs[:-8], refs[-8:]

    @pl.when(pl.program_id(0) == 0)
    def _():
        mark[...] = jnp.zeros_like(mark)
        i_hi[...], i_lo[...] = parts(inner[...])

    u_hi, u_lo = parts(jnp.concatenate([b[...] for b in blocks], axis=0))
    out[...] = c_in[...] + dot3(u_hi, u_lo, i_hi[...], i_lo[...])


def tile_of(start, size):
    return next(t for t in (1024, 512, 256, 128) if size % t == 0 and start % t == 0)


def add_inner(blocks, ucol, before, after, start, size):
    tile = tile_of(start, size)
    width, cols = blocks[0][0].shape[1], ucol.shape[1]
    first = before is None
    if first:
        before = jnp.zeros((8, 128), jnp.float32)
    rows = len(blocks) * width
    return pl.pallas_call(
        functools.partial(inner_kernel, first),
        grid=(size // tile,),
        in_specs=[
            pl.BlockSpec((tile, width), lambda i, o=(start - at) // tile: (i + o, 0)) for _, at in blocks
        ] + [
            pl.BlockSpec((tile, cols), lambda i: (i + start // tile, 0)),
            pl.BlockSpec(before.shape, lambda i: (0, 0)),
            pl.BlockSpec(memory_space=pl.ANY),
        ],
        out_specs=[pl.BlockSpec((rows, cols), lambda i: (0, 0)), pl.BlockSpec((8, 128), lambda i: (0, 0))],
        out_shape=[jax.ShapeDtypeStruct((rows, cols), jnp.float32), jax.ShapeDtypeStruct((8, 128), jnp.float32)],
        cost_estimate=pl.CostEstimate(flops=6 * size * rows * cols, bytes_accessed=4 * size * (rows + cols), transcendentals=0),
        name="inner_part",
    )(*[b for b, _ in blocks], ucol, before, after)


def write_rows(blocks, inner, c_in, out, after, start, size):
    tile = tile_of(start, size)
    width, (rows, cols) = blocks[0][0].shape[0], inner.shape
    first = out is None
    if first:
        out = jnp.zeros((8, 128), jnp.float32)
    return pl.pallas_call(
        update_kernel,
        grid=(size // tile,),
        in_specs=[
            pl.BlockSpec((width, tile), lambda i, o=(start - at) // tile: (0, i + o)) for _, at in blocks
        ] + [
            pl.BlockSpec((rows, cols), lambda i: (0, 0)),
            pl.BlockSpec((tile, cols), lambda i: (i + start // tile, 0)),
            pl.BlockSpec(memory_space=pl.ANY),
            pl.BlockSpec(memory_space=pl.ANY),
        ],
        out_specs=[
            pl.BlockSpec((tile, cols), lambda i: (i + start // tile, 0)),
            pl.BlockSpec((8, 128), lambda i: (0, 0)),
        ],
        out_shape=[
            jax.ShapeDtypeStruct(c_in.shape, jnp.float32),
            jax.ShapeDtypeStruct((8, 128), jnp.float32),
        ],
        scratch_shapes=[pltpu.VMEM((rows, cols), jnp.bfloat16)] * 2,
        input_output_aliases={} if first else {len(blocks) + 2: 0},
        cost_estimate=pl.CostEstimate(flops=6 * size * rows * cols, bytes_accessed=4 * size * (rows + 2 * cols), transcendentals=0),
        name="update_rows",
    )(*[b for b, _ in blocks], inner, c_in, out, after)


def sum_over(x, axis, n):
    if n & (n - 1) or x.shape[0] % (8 * n):
        return lax.psum(x, axis)
    me = lax.axis_index(axis)
    bits = [1 << k for k in range(n.bit_length() - 1)]
    swap = lambda y, bit: lax.ppermute(y, axis, [(i, i ^ bit) for i in range(n)])
    for bit in bits:
        up = (me & bit) != 0
        half = x.shape[0] // 2
        low, high = x[:half], x[half:]
        x = jnp.where(up, high, low) + swap(jnp.where(up, low, high), bit)
    for bit in bits[::-1]:
        up = (me & bit) != 0
        other = swap(x, bit)
        x = jnp.concatenate([jnp.where(up, other, x), jnp.where(up, x, other)], axis=0)
    return x


def ranges(units, unit):
    start = 0
    for n in units:
        yield start, n * unit
        start += n * unit


def paired(n_row, a, u, ucol, c_in):
    unit = a.shape[0] // UNITS
    over_core = lambda x: lax.ppermute(x, "pcol", [(i, i ^ 1) for i in range(4)])
    over_chip = lambda x: lax.ppermute(x, "pcol", [(i, i ^ 2) for i in range(4)])
    pieces = [lax.slice_in_dim(a, r, r + n, axis=0) for r, n in ranges(A_CHUNKS, unit)]
    pieces += [lax.slice_in_dim(u, r, r + n, axis=1) for r, n in ranges(U_CHUNKS, unit)]
    a_core = over_core(a)
    far = []
    for k, x in enumerate(pieces):
        if k >= DEPTH:
            x, far[k - DEPTH] = lax.optimization_barrier((x, far[k - DEPTH]))
        far.append(over_chip(x))
    far_a, far_u = far[:len(A_CHUNKS)], far[len(A_CHUNKS):]

    def forward(x, marks, k, last):
        if k < 2 or k < last:
            return over_core(x), jnp.zeros((8, 128), jnp.float32)
        x, mark = lax.optimization_barrier((x, marks[k - 2]))
        return over_core(x), mark

    inner, marks = None, []
    for k, (r, n) in enumerate(ranges(A_CHUNKS, unit)):
        xc, after = forward(far_a[k], marks, k, 0)
        inner, mark = add_inner([(a, 0), (a_core, 0), (far_a[k], r), (xc, r)], ucol, inner, after, r, n)
        marks.append(mark)
    u_late, _ = lax.optimization_barrier((u, marks[-2]))
    u_core = over_core(u_late)
    inner = sum_over(inner, "prow", n_row)
    out, marks = None, []
    for k, (r, n) in enumerate(ranges(U_CHUNKS, unit)):
        xc, after = forward(far_u[k], marks, k, 3)
        out, mark = write_rows([(u, 0), (u_core, 0), (far_u[k], r), (xc, r)], inner, c_in, out, after, r, n)
        marks.append(mark)
    return out


def gathered(a, u, ucol, c_in):
    a_full = lax.all_gather(a, "pcol", axis=1, tiled=True)
    u_full = lax.all_gather(u, "pcol", axis=0, tiled=True)
    dot = functools.partial(jnp.dot, precision=lax.Precision.HIGHEST, preferred_element_type=jnp.float32)
    inner = lax.psum(dot(a_full.T, ucol), "prow")
    return c_in + dot(u_full.T, inner)


def solution(mesh):
    n_row, n_col = mesh.shape["prow"], mesh.shape["pcol"]

    def on_device(a, u, ucol, c_in):
        fits = n_col == 4 and a.shape[0] % (128 * UNITS) == 0 and a.shape[1] % 128 == 0
        if fits:
            return paired(n_row, a, u, ucol, c_in)
        return gathered(a, u, ucol, c_in)

    placed = (P("prow", "pcol"), P("pcol", "prow"), P("prow", "pcol"), P("prow", "pcol"))
    return jax.shard_map(
        on_device, mesh=mesh, in_specs=placed, out_specs=P("prow", "pcol"), check_vma=False
    )
```

```python
import functools

import jax
import jax.numpy as jnp
from jax import lax
from jax.experimental import pallas as pl
from jax.experimental.pallas import tpu as pltpu
from jax.sharding import PartitionSpec as P


UNITS = 24
A_CHUNKS = (6, 6, 6, 6)
U_CHUNKS = (6, 6, 5, 3, 2, 2)
TN = (((0,), (0,)), ((), ()))


def parts(x):
    hi = x.astype(jnp.bfloat16)
    return hi, (x - hi.astype(jnp.float32)).astype(jnp.bfloat16)


def dot3(a_hi, a_lo, b_hi, b_lo):
    dot = functools.partial(lax.dot_general, dimension_numbers=TN, preferred_element_type=jnp.float32)
    return dot(a_hi, b_hi) + (dot(a_lo, b_hi) + dot(a_hi, b_lo))


def inner_kernel(first, *refs):
    blocks, (ucol, before, out) = refs[:-3], refs[-3:]

    @pl.when(pl.program_id(0) == 0)
    def _():
        out[...] = jnp.zeros_like(out) if first else before[...]

    u_hi, u_lo = parts(ucol[...])
    width = blocks[0].shape[1]
    for k, block in enumerate(blocks):
        a_hi, a_lo = parts(block[...])
        out[pl.ds(k * width, width), :] += dot3(a_hi, a_lo, u_hi, u_lo)


def update_kernel(*refs):
    blocks, (inner, c_in, _, out, i_hi, i_lo) = refs[:-6], refs[-6:]

    @pl.when(pl.program_id(0) == 0)
    def _():
        i_hi[...], i_lo[...] = parts(inner[...])

    u_hi, u_lo = parts(jnp.concatenate([b[...] for b in blocks], axis=0))
    out[...] = c_in[...] + dot3(u_hi, u_lo, i_hi[...], i_lo[...])


def tile_of(start, size):
    return next(t for t in (1024, 512, 256, 128) if size % t == 0 and start % t == 0)


def add_inner(blocks, ucol, before, start, size):
    tile = tile_of(start, size)
    width, cols = blocks[0][0].shape[1], ucol.shape[1]
    first = before is None
    if first:
        before = jnp.zeros((8, 128), jnp.float32)
    rows = len(blocks) * width
    return pl.pallas_call(
        functools.partial(inner_kernel, first),
        grid=(size // tile,),
        in_specs=[
            pl.BlockSpec((tile, width), lambda i, o=(start - at) // tile: (i + o, 0)) for _, at in blocks
        ] + [
            pl.BlockSpec((tile, cols), lambda i: (i + start // tile, 0)),
            pl.BlockSpec(before.shape, lambda i: (0, 0)),
        ],
        out_specs=pl.BlockSpec((rows, cols), lambda i: (0, 0)),
        out_shape=jax.ShapeDtypeStruct((rows, cols), jnp.float32),
        cost_estimate=pl.CostEstimate(flops=6 * size * rows * cols, bytes_accessed=4 * size * (rows + cols), transcendentals=0),
        name="inner_part",
    )(*[b for b, _ in blocks], ucol, before)


def write_rows(blocks, inner, c_in, out, start, size):
    tile = tile_of(start, size)
    width, (rows, cols) = blocks[0][0].shape[0], inner.shape
    first = out is None
    if first:
        out = jnp.zeros((8, 128), jnp.float32)
    return pl.pallas_call(
        update_kernel,
        grid=(size // tile,),
        in_specs=[
            pl.BlockSpec((width, tile), lambda i, o=(start - at) // tile: (0, i + o)) for _, at in blocks
        ] + [
            pl.BlockSpec((rows, cols), lambda i: (0, 0)),
            pl.BlockSpec((tile, cols), lambda i: (i + start // tile, 0)),
            pl.BlockSpec(memory_space=pl.ANY),
        ],
        out_specs=pl.BlockSpec((tile, cols), lambda i: (i + start // tile, 0)),
        out_shape=jax.ShapeDtypeStruct(c_in.shape, jnp.float32),
        scratch_shapes=[pltpu.VMEM((rows, cols), jnp.bfloat16)] * 2,
        input_output_aliases={} if first else {len(blocks) + 2: 0},
        cost_estimate=pl.CostEstimate(flops=6 * size * rows * cols, bytes_accessed=4 * size * (rows + 2 * cols), transcendentals=0),
        name="update_rows",
    )(*[b for b, _ in blocks], inner, c_in, out)


def sum_over(x, axis, n):
    if n & (n - 1) or x.shape[0] % (8 * n):
        return lax.psum(x, axis)
    me = lax.axis_index(axis)
    bits = [1 << k for k in range(n.bit_length() - 1)]
    swap = lambda y, bit: lax.ppermute(y, axis, [(i, i ^ bit) for i in range(n)])
    for bit in bits:
        up = (me & bit) != 0
        half = x.shape[0] // 2
        low, high = x[:half], x[half:]
        x = jnp.where(up, high, low) + swap(jnp.where(up, low, high), bit)
    for bit in bits[::-1]:
        up = (me & bit) != 0
        other = swap(x, bit)
        x = jnp.concatenate([jnp.where(up, other, x), jnp.where(up, x, other)], axis=0)
    return x


def ranges(units, unit):
    start = 0
    for n in units:
        yield start, n * unit
        start += n * unit


def paired(n_row, a, u, ucol, c_in):
    unit = a.shape[0] // UNITS
    over_core = lambda x: lax.ppermute(x, "pcol", [(i, i ^ 1) for i in range(4)])
    over_chip = lambda x: lax.ppermute(x, "pcol", [(i, i ^ 2) for i in range(4)])

    a_ranges, u_ranges = list(ranges(A_CHUNKS, unit)), list(ranges(U_CHUNKS, unit))
    head = lax.slice_in_dim(a, 0, a_ranges[0][1], axis=0)
    head, a_rest, u_rest = lax.optimization_barrier((head, a, u))
    far_a = [over_chip(head)]
    for k, (r, n) in enumerate(a_ranges[1:], 1):
        far_a.append(over_chip(lax.slice_in_dim(a_rest, r, r + n, axis=0)))
    far_u = [over_chip(lax.slice_in_dim(u_rest, r, r + n, axis=1)) for r, n in u_ranges]

    a_core = over_core(a)
    inner = None
    for k, (r, n) in enumerate(a_ranges):
        xc = over_core(far_a[k])
        inner = add_inner([(a, 0), (a_core, 0), (far_a[k], r), (xc, r)], ucol, inner, r, n)
    u_core = over_core(u)
    inner = sum_over(inner, "prow", n_row)
    out = None
    for k, (r, n) in enumerate(u_ranges):
        xc = over_core(far_u[k])
        out = write_rows([(u, 0), (u_core, 0), (far_u[k], r), (xc, r)], inner, c_in, out, r, n)
    return out


def gathered(a, u, ucol, c_in):
    a_full = lax.all_gather(a, "pcol", axis=1, tiled=True)
    u_full = lax.all_gather(u, "pcol", axis=0, tiled=True)
    dot = functools.partial(jnp.dot, precision=lax.Precision.HIGHEST, preferred_element_type=jnp.float32)
    inner = lax.psum(dot(a_full.T, ucol), "prow")
    return c_in + dot(u_full.T, inner)


def solution(mesh):
    n_row, n_col = mesh.shape["prow"], mesh.shape["pcol"]
    two_chips = n_col == 4

    def on_device(a, u, ucol, c_in):
        if two_chips and a.shape[0] % (128 * UNITS) == 0 and a.shape[1] % 128 == 0:
            return paired(n_row, a, u, ucol, c_in)
        return gathered(a, u, ucol, c_in)

    placed = (P("prow", "pcol"), P("pcol", "prow"), P("prow", "pcol"), P("prow", "pcol"))
    return jax.shard_map(
        on_device, mesh=mesh, in_specs=placed, out_specs=P("prow", "pcol"), check_vma=False
    )
```

```python
import functools

import jax
import jax.numpy as jnp
from jax import lax
from jax.experimental import pallas as pl
from jax.experimental.pallas import tpu as pltpu
from jax.sharding import PartitionSpec as P


UNITS = 24
A_CHUNKS = (1, 5, 6, 6, 4, 2)
U_CHUNKS = (6, 6, 5, 4, 2, 1)
TN = (((0,), (0,)), ((), ()))


def parts(x):
    hi = x.astype(jnp.bfloat16)
    return hi, (x - hi.astype(jnp.float32)).astype(jnp.bfloat16)


def dot3(a_hi, a_lo, b_hi, b_lo):
    dot = functools.partial(lax.dot_general, dimension_numbers=TN, preferred_element_type=jnp.float32)
    return dot(a_hi, b_hi) + (dot(a_lo, b_hi) + dot(a_hi, b_lo))


def inner_kernel(first, *refs):
    blocks, (ucol, before, out) = refs[:-3], refs[-3:]

    @pl.when(pl.program_id(0) == 0)
    def _():
        out[...] = jnp.zeros_like(out) if first else before[...]

    u_hi, u_lo = parts(ucol[...])
    width = blocks[0].shape[1]
    for k, block in enumerate(blocks):
        a_hi, a_lo = parts(block[...])
        out[pl.ds(k * width, width), :] += dot3(a_hi, a_lo, u_hi, u_lo)


def update_kernel(*refs):
    blocks, (inner, c_in, _, out, i_hi, i_lo) = refs[:-6], refs[-6:]

    @pl.when(pl.program_id(0) == 0)
    def _():
        i_hi[...], i_lo[...] = parts(inner[...])

    u_hi, u_lo = parts(jnp.concatenate([b[...] for b in blocks], axis=0))
    out[...] = c_in[...] + dot3(u_hi, u_lo, i_hi[...], i_lo[...])


def tile_of(start, size):
    sizes = (512, 256, 128) if size > 1024 else (256, 128)
    return next(t for t in sizes if size % t == 0 and start % t == 0)


def add_inner(blocks, ucol, before, start, size):
    tile = tile_of(start, size)
    width, cols = blocks[0][0].shape[1], ucol.shape[1]
    first = before is None
    if first:
        before = jnp.zeros((8, 128), jnp.float32)
    rows = len(blocks) * width
    return pl.pallas_call(
        functools.partial(inner_kernel, first),
        grid=(size // tile,),
        in_specs=[
            pl.BlockSpec((tile, width), lambda i, o=(start - at) // tile: (i + o, 0)) for _, at in blocks
        ] + [
            pl.BlockSpec((tile, cols), lambda i: (i + start // tile, 0)),
            pl.BlockSpec(before.shape, lambda i: (0, 0)),
        ],
        out_specs=pl.BlockSpec((rows, cols), lambda i: (0, 0)),
        out_shape=jax.ShapeDtypeStruct((rows, cols), jnp.float32),
        cost_estimate=pl.CostEstimate(flops=6 * size * rows * cols, bytes_accessed=4 * size * (rows + cols), transcendentals=0),
        name="inner_part",
    )(*[b for b, _ in blocks], ucol, before)


def write_rows(blocks, inner, c_in, out, start, size):
    tile = tile_of(start, size)
    width, (rows, cols) = blocks[0][0].shape[0], inner.shape
    first = out is None
    if first:
        out = jnp.zeros((8, 128), jnp.float32)
    return pl.pallas_call(
        update_kernel,
        grid=(size // tile,),
        in_specs=[
            pl.BlockSpec((width, tile), lambda i, o=(start - at) // tile: (0, i + o)) for _, at in blocks
        ] + [
            pl.BlockSpec((rows, cols), lambda i: (0, 0)),
            pl.BlockSpec((tile, cols), lambda i: (i + start // tile, 0)),
            pl.BlockSpec(memory_space=pl.ANY),
        ],
        out_specs=pl.BlockSpec((tile, cols), lambda i: (i + start // tile, 0)),
        out_shape=jax.ShapeDtypeStruct(c_in.shape, jnp.float32),
        scratch_shapes=[pltpu.VMEM((rows, cols), jnp.bfloat16)] * 2,
        input_output_aliases={} if first else {len(blocks) + 2: 0},
        cost_estimate=pl.CostEstimate(flops=6 * size * rows * cols, bytes_accessed=4 * size * (rows + 2 * cols), transcendentals=0),
        name="update_rows",
    )(*[b for b, _ in blocks], inner, c_in, out)


def sum_over(x, axis, n):
    if n & (n - 1) or x.shape[0] % (8 * n):
        return lax.psum(x, axis)
    me = lax.axis_index(axis)
    bits = [1 << k for k in range(n.bit_length() - 1)]
    swap = lambda y, bit: lax.ppermute(y, axis, [(i, i ^ bit) for i in range(n)])
    for bit in bits:
        up = (me & bit) != 0
        half = x.shape[0] // 2
        low, high = x[:half], x[half:]
        x = jnp.where(up, high, low) + swap(jnp.where(up, low, high), bit)
    for bit in bits[::-1]:
        up = (me & bit) != 0
        other = swap(x, bit)
        x = jnp.concatenate([jnp.where(up, other, x), jnp.where(up, x, other)], axis=0)
    return x


def ranges(units, unit):
    start = 0
    for n in units:
        yield start, n * unit
        start += n * unit


def paired(n_row, a, u, ucol, c_in):
    unit = a.shape[0] // UNITS
    over_core = lambda x: lax.ppermute(x, "pcol", [(i, i ^ 1) for i in range(4)])
    over_chip = lambda x: lax.ppermute(x, "pcol", [(i, i ^ 2) for i in range(4)])

    a_ranges, u_ranges = list(ranges(A_CHUNKS, unit)), list(ranges(U_CHUNKS, unit))
    far_a, a_rest, u_rest = [], a, u
    for k, (r, n) in enumerate(a_ranges):
        piece = lax.slice_in_dim(a_rest, r, r + n, axis=0)
        if k < 2:
            piece, a_rest, u_rest = lax.optimization_barrier((piece, a_rest, u_rest))
        far_a.append(over_chip(piece))
    far_u = [over_chip(lax.slice_in_dim(u_rest, r, r + n, axis=1)) for r, n in u_ranges]

    a_core = over_core(a)
    inner = None
    for k, (r, n) in enumerate(a_ranges):
        xc = over_core(far_a[k])
        inner = add_inner([(a, 0), (a_core, 0), (far_a[k], r), (xc, r)], ucol, inner, r, n)
    u_core = over_core(u)
    inner = sum_over(inner, "prow", n_row)
    out = None
    for k, (r, n) in enumerate(u_ranges):
        xc = over_core(far_u[k])
        out = write_rows([(u, 0), (u_core, 0), (far_u[k], r), (xc, r)], inner, c_in, out, r, n)
    return out


def gathered(a, u, ucol, c_in):
    a_full = lax.all_gather(a, "pcol", axis=1, tiled=True)
    u_full = lax.all_gather(u, "pcol", axis=0, tiled=True)
    dot = functools.partial(jnp.dot, precision=lax.Precision.HIGHEST, preferred_element_type=jnp.float32)
    inner = lax.psum(dot(a_full.T, ucol), "prow")
    return c_in + dot(u_full.T, inner)


def solution(mesh):
    n_row, n_col = mesh.shape["prow"], mesh.shape["pcol"]
    two_chips = n_col == 4

    def on_device(a, u, ucol, c_in):
        if two_chips and a.shape[0] % (128 * UNITS) == 0 and a.shape[1] % 128 == 0:
            return paired(n_row, a, u, ucol, c_in)
        return gathered(a, u, ucol, c_in)

    placed = (P("prow", "pcol"), P("pcol", "prow"), P("prow", "pcol"), P("prow", "pcol"))
    return jax.shard_map(
        on_device, mesh=mesh, in_specs=placed, out_specs=P("prow", "pcol"), check_vma=False
    )
```
